32 devices in a mesh: rep: 4 (over y, x), tp: 8 (over z, core).
Axes of the slice: x: 2, y: 2, z: 4, core: 2. Of those that a mesh axis runs over, the one named last changes fastest.
Arguments:
- deltas: bfloat16 [4, 3, 4096, 8192], P('rep', None, 'tp'), may hold values from -2600 to 2600
- staleness: int32 [4], P('rep'), may hold values from 0 to 2
Outputs:
- update: bfloat16 [4096, 8192], P('tp')
The draws below stay inside these ranges and needn't reach their ends.
All inputs are finite; a program needn't handle non-finite values.
Results may differ from the reference program's by a relative error of at most 0.028.
Values may be sent and summed in bfloat16 or wider, within the bound.
A program may use at most 128 MiB of HBM per device.

```python
import jax
import jax.numpy as jnp
from jax import lax

ROWS = 4096
COLS = 8192
TILE = 512
SNAPS = 3
NS_ITERS = 5
REPLICAS = 4
N_REP = 4


def draw_deltas(key, part):
    keys = jax.random.split(key, 3)
    base = jax.random.truncated_normal(keys[0], -6.0, 6.0, (REPLICAS, SNAPS, ROWS, COLS), jnp.float32)
    replica_scale = 3.0 ** (jnp.arange(REPLICAS, dtype=jnp.float32) / max(REPLICAS - 1, 1))
    row_scale = jax.random.uniform(keys[1], (ROWS,), jnp.float32, 0.5, 2.0)
    col_scale = jax.random.uniform(keys[2], (COLS,), jnp.float32, 0.5, 2.0)
    mixed = base
    values = mixed * row_scale[:, None] * col_scale[None, :] * replica_scale[:, None, None, None]
    return values.astype(jnp.bfloat16)


def place_ends(entries, own_key, smallest, high):
    dims = entries.shape
    index_at = [jax.random.randint(jax.random.fold_in(own_key, axis), (), 0, dims[axis]) for axis in range(len(dims))]
    entries = entries.at[tuple(index_at)].set(smallest)
    longest = dims.index(max(dims))
    index_at[longest] = (index_at[longest] + 1) % dims[longest]
    return entries.at[tuple(index_at)].set(high)


def setup_inputs(seed: int = 0) -> dict:
    seeds = jax.random.split(jax.random.key(seed), 3)
    return {
        "deltas": draw_deltas(jax.random.fold_in(seeds[2], 71), 0),
        "staleness": place_ends(jax.random.randint(seeds[1], (REPLICAS,), 0, SNAPS), jax.random.fold_in(seeds[1], 1), 0, SNAPS - 1).astype(jnp.int32),
    }


damping = 0.001

def newton_root(stat):
    identity = jnp.eye(TILE, dtype=jnp.float32)
    frob_norm = jnp.sqrt(jnp.sum(stat * stat))
    current = stat / frob_norm
    iterate = identity
    for step in range(NS_ITERS):
        factor = (5.0 * identity - current) * 0.25
        iterate = jnp.dot(iterate, factor, precision=lax.Precision.HIGHEST, preferred_element_type=jnp.float32)
        if step + 1 < NS_ITERS:
            square = jnp.dot(factor, factor, precision=lax.Precision.HIGHEST, preferred_element_type=jnp.float32)
            fourth = jnp.dot(square, square, precision=lax.Precision.HIGHEST, preferred_element_type=jnp.float32)
            current = jnp.dot(fourth, current, precision=lax.Precision.HIGHEST, preferred_element_type=jnp.float32)
    return (iterate * frob_norm ** (-0.25)).astype(jnp.bfloat16)

def reference(deltas, staleness):
    picked = deltas[jnp.arange(REPLICAS), staleness]
    mean_delta = (lax.optimization_barrier(jnp.sum(picked.astype(jnp.float32), axis=0)) / N_REP).astype(jnp.bfloat16)
    row_blocks = ROWS // TILE
    col_blocks = COLS // TILE
    identity = jnp.eye(TILE, dtype=jnp.float32)

    def tile_update(index):
        row_start = (index // col_blocks * TILE).astype(jnp.int32)
        col_start = (index % col_blocks * TILE).astype(jnp.int32)
        block = lax.dynamic_slice(picked, (jnp.int32(0), row_start, col_start), (REPLICAS, TILE, TILE)).astype(jnp.float32)
        left_gram = jnp.einsum('rij,rkj->ik', block, block, precision=lax.Precision.HIGHEST)
        right_gram = jnp.einsum('rji,rjk->ik', block, block, precision=lax.Precision.HIGHEST)
        left_root = newton_root(left_gram / (N_REP * TILE) + damping * identity)
        right_root = newton_root(right_gram / (N_REP * TILE) + damping * identity)
        mean_tile = lax.dynamic_slice(mean_delta, (row_start, col_start), (TILE, TILE))
        half_product = jnp.dot(left_root, mean_tile, preferred_element_type=jnp.float32).astype(jnp.bfloat16)
        return jnp.dot(half_product, right_root, preferred_element_type=jnp.float32).astype(jnp.bfloat16)
    tiles = lax.map(tile_update, jnp.arange(row_blocks * col_blocks, dtype=jnp.int32))
    return tiles.reshape(row_blocks, col_blocks, TILE, TILE).transpose(0, 2, 1, 3).reshape(ROWS, COLS)
```

```python
import jax
import jax.numpy as jnp
from jax import lax
from jax.sharding import PartitionSpec as P

TILE = 512
NS_ITERS = 5


damping = 0.001


def bf(values):
    return values.astype(jnp.bfloat16)


def multiply(left_side, right_side):
    return jnp.einsum(
        "xij,xjk->xik", bf(left_side), bf(right_side), preferred_element_type=jnp.float32
    )


def inverse_roots(stat_stack):
    identity = jnp.eye(TILE, dtype=jnp.float32)
    frob_norm = jnp.sqrt(jnp.sum(stat_stack * stat_stack, axis=(1, 2), keepdims=True))
    quarter = stat_stack * (0.25 / frob_norm)
    missing = quarter
    scale = 1.25
    square_scale = 1.25 * 1.25
    for _ in range(NS_ITERS - 1):
        square = 2.5 * quarter - multiply(quarter, quarter)
        fourth = 2.0 * square_scale * square - multiply(square, square)
        quarter = square_scale * square_scale * quarter - multiply(fourth, quarter)
        missing = 1.25 * missing + scale * quarter - multiply(missing, quarter)
        scale = scale * 1.25
    return bf((scale * identity - missing) * frob_norm ** (-0.25))


def to_grid(strip_rows, tile):
    return strip_rows.reshape(
        strip_rows.shape[0] // tile, tile, strip_rows.shape[1] // tile, tile
    ).transpose(0, 2, 1, 3)


def to_strip(tile_grid):
    grid_rows, grid_cols, tile, _ = tile_grid.shape
    return tile_grid.transpose(0, 2, 1, 3).reshape(grid_rows * tile, grid_cols * tile)


def precondition(root_grid, mean_tiles):
    half_product = bf(jnp.einsum(
        "abij,abjk->abik", root_grid[:, :, 0], mean_tiles, preferred_element_type=jnp.float32
    ))
    return bf(jnp.einsum(
        "abij,abjk->abik", half_product, root_grid[:, :, 1], preferred_element_type=jnp.float32
    ))


def by_strips(picked, replicas):
    column_strip = lax.all_to_all(picked, "tp", split_axis=1, concat_axis=0, tiled=True)
    grid_rows = column_strip.shape[0] // TILE
    grid_cols = column_strip.shape[1] // TILE
    own_rows = grid_rows // replicas
    tile_set = to_grid(column_strip, TILE)
    left_gram = jnp.einsum(
        "abik,abjk->abij", tile_set, tile_set, preferred_element_type=jnp.float32
    )
    right_gram = jnp.einsum(
        "abki,abkj->abij", tile_set, tile_set, preferred_element_type=jnp.float32
    )
    gram_stack = jnp.stack([left_gram, right_gram], axis=2).reshape(
        grid_rows * grid_cols * 2, TILE, TILE
    )
    gram_sums, strip_sum = (
        lax.psum_scatter(
            bf(gram_stack), "rep", scatter_dimension=0, tiled=True
        ).astype(jnp.float32),
        lax.psum_scatter(
            column_strip, "rep", scatter_dimension=0, tiled=True
        ).astype(jnp.float32),
    )
    mean_part = bf(strip_sum / replicas)
    identity = jnp.eye(TILE, dtype=jnp.float32)
    root_stack = inverse_roots(gram_sums / (replicas * TILE) + damping * identity)
    local_tiles = precondition(
        root_stack.reshape(own_rows, grid_cols, 2, TILE, TILE), to_grid(mean_part, TILE)
    )
    gathered = lax.all_gather(to_strip(local_tiles), "rep", axis=0, tiled=True)
    return lax.all_to_all(gathered, "tp", split_axis=0, concat_axis=1, tiled=True)


def by_rows(picked, replicas):
    rows, cols = picked.shape
    own = cols // replicas
    blocks = picked.reshape(rows, replicas, own).transpose(1, 0, 2)
    blocks = lax.all_to_all(blocks, "rep", split_axis=0, concat_axis=0, tiled=True)
    tile_set = blocks.reshape(
        replicas, rows // TILE, TILE, own // TILE, TILE
    ).transpose(1, 3, 0, 2, 4)
    left_gram = jnp.einsum(
        "abrik,abrjk->abij", tile_set, tile_set, preferred_element_type=jnp.float32
    )
    right_gram = jnp.einsum(
        "abrki,abrkj->abij", tile_set, tile_set, preferred_element_type=jnp.float32
    )
    mean_tiles = bf(jnp.sum(tile_set.astype(jnp.float32), axis=2) / replicas)
    identity = jnp.eye(TILE, dtype=jnp.float32)
    stats = jnp.stack([left_gram, right_gram], axis=2) / (replicas * TILE) + damping * identity
    roots = inverse_roots(stats.reshape(-1, TILE, TILE)).reshape(stats.shape)
    strip = to_strip(precondition(roots, mean_tiles))
    return lax.all_gather(strip, "rep", axis=1, tiled=True)


def local(deltas, staleness):
    replicas = lax.axis_size("rep")
    picked = lax.dynamic_index_in_dim(deltas[0], staleness[0], 0, keepdims=False)
    rows, cols = picked.shape
    if rows % TILE == 0 and cols % (replicas * TILE) == 0:
        return by_rows(picked, replicas)
    return by_strips(picked, replicas)


def solution(mesh):
    return jax.shard_map(
        local,
        mesh=mesh,
        in_specs=(P("rep", None, "tp", None), P("rep")),
        out_specs=P("tp", None),
        check_vma=False,
    )
```

```python
import functools

import jax
import jax.numpy as jnp
from jax import lax
from jax.experimental import pallas as pl
from jax.experimental.pallas import tpu as pltpu
from jax.sharding import PartitionSpec as P

TILE = 512
NS_ITERS = 5


damping = 0.001


def bf(values):
    return values.astype(jnp.bfloat16)


def multiply(left_side, right_side):
    return jnp.einsum(
        "xij,xjk->xik", bf(left_side), bf(right_side), preferred_element_type=jnp.float32
    )


def inverse_roots(stat_stack):
    identity = jnp.eye(TILE, dtype=jnp.float32)
    frob_norm = jnp.sqrt(jnp.sum(stat_stack * stat_stack, axis=(1, 2), keepdims=True))
    quarter = stat_stack * (0.25 / frob_norm)
    missing = quarter
    scale = 1.25
    square_scale = 1.25 * 1.25
    for _ in range(NS_ITERS - 1):
        square = 2.5 * quarter - multiply(quarter, quarter)
        fourth = 2.0 * square_scale * square - multiply(square, square)
        quarter = square_scale * square_scale * quarter - multiply(fourth, quarter)
        missing = 1.25 * missing + scale * quarter - multiply(missing, quarter)
        scale = scale * 1.25
    return bf((scale * identity - missing) * frob_norm ** (-0.25))


def to_grid(strip_rows, tile):
    return strip_rows.reshape(
        strip_rows.shape[0] // tile, tile, strip_rows.shape[1] // tile, tile
    ).transpose(0, 2, 1, 3)


def to_strip(tile_grid):
    grid_rows, grid_cols, tile, _ = tile_grid.shape
    return tile_grid.transpose(0, 2, 1, 3).reshape(grid_rows * tile, grid_cols * tile)


def precondition(root_grid, mean_tiles):
    half_product = bf(jnp.einsum(
        "abij,abjk->abik", root_grid[:, :, 0], mean_tiles, preferred_element_type=jnp.float32
    ))
    return bf(jnp.einsum(
        "abij,abjk->abik", half_product, root_grid[:, :, 1], preferred_element_type=jnp.float32
    ))


def by_strips(picked, replicas):
    column_strip = lax.all_to_all(picked, "tp", split_axis=1, concat_axis=0, tiled=True)
    grid_rows = column_strip.shape[0] // TILE
    grid_cols = column_strip.shape[1] // TILE
    own_rows = grid_rows // replicas
    tile_set = to_grid(column_strip, TILE)
    left_gram = jnp.einsum(
        "abik,abjk->abij", tile_set, tile_set, preferred_element_type=jnp.float32
    )
    right_gram = jnp.einsum(
        "abki,abkj->abij", tile_set, tile_set, preferred_element_type=jnp.float32
    )
    gram_stack = jnp.stack([left_gram, right_gram], axis=2).reshape(
        grid_rows * grid_cols * 2, TILE, TILE
    )
    gram_sums, strip_sum = (
        lax.psum_scatter(
            bf(gram_stack), "rep", scatter_dimension=0, tiled=True
        ).astype(jnp.float32),
        lax.psum_scatter(
            column_strip, "rep", scatter_dimension=0, tiled=True
        ).astype(jnp.float32),
    )
    mean_part = bf(strip_sum / replicas)
    identity = jnp.eye(TILE, dtype=jnp.float32)
    root_stack = inverse_roots(gram_sums / (replicas * TILE) + damping * identity)
    local_tiles = precondition(
        root_stack.reshape(own_rows, grid_cols, 2, TILE, TILE), to_grid(mean_part, TILE)
    )
    gathered = lax.all_gather(to_strip(local_tiles), "rep", axis=0, tiled=True)
    return lax.all_to_all(gathered, "tp", split_axis=0, concat_axis=1, tiled=True)


BLOCK = 256
AHEAD = 2
RELAY = True
COMPUTE = True


def product(left_side, right_side, contract=((1,), (0,))):
    return lax.dot_general(
        left_side, right_side, (contract, ((), ())), preferred_element_type=jnp.float32
    )


def tile_root(quarter, square, fourth, missing, norms):
    blocks = [pl.ds(start, BLOCK) for start in range(0, TILE, BLOCK)]

    def step(_, scale):
        first = 1.25 * 1.25
        for side in range(2):
            for rows in blocks:
                mine = quarter[side, rows, :]
                square[side, rows, :] = bf(2.5 * mine - product(mine, quarter[side]))
        for side in range(2):
            for rows in blocks:
                mine = square[side, rows, :]
                fourth[side, rows, :] = bf(2.0 * first * mine - product(mine, square[side]))
        for side in range(2):
            for rows in blocks:
                mine = quarter[side, rows, :]
                quarter[side, rows, :] = bf(first * first * mine - product(mine, fourth[side]))
        for side in range(2):
            for rows in blocks:
                mine = missing[side, rows, :]
                missing[side, rows, :] = bf(
                    1.25 * mine + scale * quarter[side, rows, :] - product(mine, quarter[side])
                )
        return scale * 1.25

    scale = lax.fori_loop(0, NS_ITERS - 1, step, jnp.float32(1.25))
    for side in range(2):
        for start, rows in zip(range(0, TILE, BLOCK), blocks):
            row = lax.broadcasted_iota(jnp.int32, (BLOCK, TILE), 0) + start
            col = lax.broadcasted_iota(jnp.int32, (BLOCK, TILE), 1)
            full = jnp.where(row == col, scale, 0.0) - missing[side, rows, :]
            square[side, rows, :] = bf(full * norms[side])


def tile_update(parts, out_ref, count, gram, quarter, square, fourth, missing):
    starts = range(0, TILE, BLOCK)
    norms = []
    for side in range(2):
        total = jnp.zeros((1, 1), jnp.float32)
        for start in starts:
            rows = pl.ds(start, BLOCK)
            acc = None
            for r in range(count):
                if side == 0:
                    term = product(parts[r, rows, :], parts[r], ((1,), (1,)))
                else:
                    term = product(parts[r, :, rows], parts[r], ((0,), (0,)))
                acc = term if acc is None else acc + term
            row = lax.broadcasted_iota(jnp.int32, (BLOCK, TILE), 0) + start
            col = lax.broadcasted_iota(jnp.int32, (BLOCK, TILE), 1)
            acc = acc * (1.0 / (count * TILE)) + jnp.where(row == col, damping, 0.0)
            gram[side, rows, :] = acc
            total = total + jnp.sum(
                jnp.sum(acc * acc, axis=0, keepdims=True), axis=1, keepdims=True
            )
        for start in starts:
            rows = pl.ds(start, BLOCK)
            value = bf(gram[side, rows, :] * (0.25 * lax.rsqrt(total)))
            quarter[side, rows, :] = value
            missing[side, rows, :] = value
        norms.append(lax.rsqrt(jnp.sqrt(jnp.sqrt(total))))
    tile_root(quarter, square, fourth, missing, norms)
    for start in starts:
        rows = pl.ds(start, BLOCK)
        total = parts[0, rows, :].astype(jnp.float32)
        for r in range(1, count):
            total = total + parts[r, rows, :].astype(jnp.float32)
        fourth[0, rows, :] = bf(total * (1.0 / count))
    for start in starts:
        rows = pl.ds(start, BLOCK)
        half = bf(product(square[0, rows, :], fourth[0]))
        out_ref[rows, :] = bf(product(half, square[1]))


def exchange_kernel(
    count, picked, out_ref, parts, tiles, gram, quarter, square, fourth,
    missing, in_send, in_recv, in_copy, out_send, out_recv, out_copy, hop_send, hop_recv,
):
    me = lax.axis_index("rep")
    rows, cols = out_ref.shape
    across = cols // TILE // count
    own = rows // TILE * across
    relay = RELAY and count == 4
    mid = TILE // 2

    def peer(k):
        return me ^ k if count & (count - 1) == 0 else lax.rem(me + k, count)

    def source(k):
        return me ^ k if count & (count - 1) == 0 else lax.rem(me + count - k, count)

    def place(ref, owner, t, start=0, size=TILE):
        top = pl.multiple_of(t // across * TILE + start, size)
        left = pl.multiple_of((owner * across + lax.rem(t, across)) * TILE, TILE)
        return ref.at[pl.ds(top, size), pl.ds(left, TILE)]

    def inward(t, k):
        to = peer(k)
        return pltpu.make_async_remote_copy(
            src_ref=place(picked, to, t), dst_ref=parts.at[t, me],
            send_sem=in_send.at[t, k], recv_sem=in_recv.at[t, k],
            device_id={"rep": to}, device_id_type=pl.DeviceIdType.MESH,
        )

    def inward_own(t):
        return pltpu.make_async_copy(place(picked, me, t), parts.at[t, me], in_copy.at[t])

    def outward(t, k):
        to = peer(k)
        return pltpu.make_async_remote_copy(
            src_ref=tiles.at[t], dst_ref=place(out_ref, me, t),
            send_sem=out_send.at[t, k], recv_sem=out_recv.at[t, k],
            device_id={"rep": to}, device_id_type=pl.DeviceIdType.MESH,
        )

    def outward_own(t):
        return pltpu.make_async_copy(tiles.at[t], place(out_ref, me, t), out_copy.at[t])

    def hop(t, k):
        half = place(out_ref, me ^ k, t, (k - 1) * mid, mid)
        return pltpu.make_async_remote_copy(
            src_ref=half, dst_ref=half,
            send_sem=hop_send.at[t, k], recv_sem=hop_recv.at[t, k],
            device_id={"rep": me ^ (3 - k)}, device_id_type=pl.DeviceIdType.MESH,
        )

    direct = range(1, 3) if relay else range(1, count)

    def send_in(t):
        for k in range(1, count):
            inward(t, k).start()
        inward_own(t).start()

    def forward(t):
        for k in (1, 2):
            outward(t, k).wait_recv()
            hop(t, k).start()

    barrier = pltpu.get_barrier_semaphore()
    for k in range(1, count):
        pl.semaphore_signal(
            barrier, inc=1, device_id={"rep": peer(k)}, device_id_type=pl.DeviceIdType.MESH
        )
    pl.semaphore_wait(barrier, count - 1)

    for t in range(min(AHEAD, own)):
        send_in(t)

    @pl.loop(0, own)
    def _(t):
        inward_own(t).wait()
        for k in range(1, count):
            inward(t, k).wait()

        @pl.when(t + AHEAD < own)
        def _():
            send_in(t + AHEAD)

        if COMPUTE:
            tile_update(
                parts.at[t], tiles.at[t], count, gram, quarter, square, fourth, missing
            )
        for k in direct:
            outward(t, k).start()
        outward_own(t).start()
        if relay:

            @pl.when(t > 0)
            def _():
                forward(t - 1)

    if relay:
        forward(own - 1)

    @pl.loop(0, own)
    def _(t):
        outward_own(t).wait()
        for k in direct:
            outward(t, k).wait_send()
            if not relay:
                outward(t, k).wait_recv()
        if relay:
            for k in (1, 2):
                hop(t, k).wait()


def by_rows(picked, replicas):
    rows, cols = picked.shape
    own = (rows // TILE) * (cols // TILE // replicas)
    square = pltpu.VMEM((2, TILE, TILE), jnp.bfloat16)
    pairs = pltpu.SemaphoreType.DMA((own, replicas))
    single = pltpu.SemaphoreType.DMA((own,))
    flops = own * (2 * replicas + 34) * 2 * TILE**3
    return pl.pallas_call(
        functools.partial(exchange_kernel, replicas),
        out_shape=jax.ShapeDtypeStruct((rows, cols), jnp.bfloat16),
        in_specs=[
            pl.BlockSpec(memory_space=pl.ANY),
        ],
        out_specs=pl.BlockSpec(memory_space=pl.ANY),
        scratch_shapes=[
            pltpu.VMEM((own, replicas, TILE, TILE), jnp.bfloat16),
            pltpu.VMEM((own, TILE, TILE), jnp.bfloat16),
            pltpu.VMEM((2, TILE, TILE), jnp.float32),
            square, square, square, square,
            pairs, pairs, single, pairs, pairs, single, pairs, pairs,
        ],
        compiler_params=pltpu.CompilerParams(
            collective_id=0, has_side_effects=True, vmem_limit_bytes=60 * 1024 * 1024
        ),
        cost_estimate=pl.CostEstimate(
            flops=flops, bytes_accessed=4 * rows * cols, transcendentals=0
        ),
    )(picked)


def local(deltas, staleness):
    replicas = lax.axis_size("rep")
    picked = lax.dynamic_index_in_dim(deltas[0], staleness[0], 0, keepdims=False)
    rows, cols = picked.shape
    if rows % TILE == 0 and cols % (replicas * TILE) == 0:
        return by_rows(picked, replicas)
    return by_strips(picked, replicas)


def solution(mesh):
    return jax.shard_map(
        local,
        mesh=mesh,
        in_specs=(P("rep", None, "tp", None), P("rep")),
        out_specs=P("tp", None),
        check_vma=False,
    )
```
